256 devices in a mesh: bgrp: 16 (over y, z_lo, core), clane: 16 (over z_hi, x).
Axes of the slice: x: 4, y: 4, z: 8 (z_hi: 4, z_lo: 2; z = z_hi * 2 + z_lo), core: 2. Of those that a mesh axis runs over, the one named last changes fastest.
Arguments:
- amplitudes: bfloat16 [512, 512], P('bgrp', 'clane'), may hold values from -1.1953125 to 1.1953125
- integrals: bfloat16 [4, 512, 512, 512], P(None, 'bgrp', 'clane'), may hold values from -0.25 to 0.25
- couplings: bfloat16 [4, 512, 512, 512], P(None, 'bgrp', 'clane'), may hold values from -0.25 to 0.25
- virtual_energy: float32 [512], replicated, may hold values from 0.5 to 3
- sector_labels: int32 [512], replicated, may hold values from 0 to 7
- sector_shift: float32 [8], replicated, may hold values from 0.5 to 4
- occupied_energy: float32 [64], replicated, may hold values from -3 to -1
- pair_orbitals: int32 [2], replicated, may hold values from 0 to 63
- third_orbitals: int32 [4], replicated, may hold values from 0 to 63
Outputs:
- residual: float32 [512, 512], P('bgrp', 'clane')
The draws below stay inside these ranges and needn't reach their ends.
All inputs are finite; a program needn't handle non-finite values.
Results may differ from the reference program's by a relative error of at most 0.0041.
Values may be sent and summed in bfloat16 or wider, within the bound.
No kernel may reach another device: no remote copies, remote signals or barrier semaphores. Data moves between devices by JAX's collectives and lax.ppermute only.
A program may use at most 128 MiB of HBM per device.

```python
import math
import jax
import jax.numpy as jnp
from jax import lax

A = 512
NOCC = 64
NSECT = 8
K = 4


def set_ends(drawn, rng, low, largest):
    longest = drawn.shape.index(max(drawn.shape))
    spots = []
    for shift in (0, 1):
        where = [jax.random.randint(jax.random.fold_in(rng, axis), (), 0, length) for axis, length in enumerate(drawn.shape)]
        where[longest] = (where[longest] + shift) % drawn.shape[longest]
        spots.append(tuple(where))
    return drawn.at[spots[0]].set(low).at[spots[1]].set(largest)


def block_scale(stream_key, dims, split, smallest, top_value):
    factor_of = 1.0
    for dim, parts in split:
        heights = jax.random.uniform(jax.random.fold_in(jax.random.fold_in(stream_key, 6), dim), (parts,), jnp.float32, smallest / len(split), top_value / len(split))
        factor_of = factor_of * jnp.repeat(jnp.exp(heights), dims[dim] // parts).reshape((-1,) + (1,) * (len(dims) - 1 - dim))
    return factor_of


def normal_values(key, extent, deviation, most, cuts=(), kind=jnp.bfloat16):
    drawn = deviation * jax.random.normal(key, extent, jnp.float32)
    if cuts:
        drawn = drawn * block_scale(key, extent, cuts, -0.22, 0.18)
    return jnp.clip(drawn, -most, most).astype(kind)


def setup_inputs(seed: int = 0) -> dict:
    key_list = jax.random.split(jax.random.key(seed), 10)
    amplitudes = normal_values(key_list[0], (A, A), 0.2, 1.1953125, ((0, 16), (1, 16)))
    integrals = normal_values(key_list[1], (K, A, A, A), A ** -0.5, 0.25, ((1, 16), (2, 16)))
    couplings = normal_values(key_list[2], (K, A, A, A), A ** -0.5, 0.25, ((1, 16), (2, 16)))
    virtual_energy = jnp.clip(jax.random.uniform(key_list[3], (A,), jnp.float32, 0.5, 3.0), 0.5, 3.0)
    sector_labels = set_ends(jax.random.randint(key_list[4], (A,), 0, NSECT), jax.random.fold_in(key_list[4], 1), 0, NSECT - 1).astype(jnp.int32)
    sector_shift = jnp.clip(jnp.exp(jax.random.uniform(key_list[5], (NSECT,), jnp.float32, math.log(0.5), math.log(4.0))), 0.5, 4.0)
    occupied_energy = jnp.clip(jax.random.uniform(key_list[6], (NOCC,), jnp.float32, -3.0, -1.0), -3.0, -1.0)
    pair_orbitals = jax.random.randint(key_list[7], (2,), 0, NOCC).astype(jnp.int32)
    third_orbitals = set_ends(jax.random.randint(key_list[8], (K,), 0, NOCC), jax.random.fold_in(key_list[8], 1), 0, NOCC - 1).astype(jnp.int32)
    return dict(amplitudes=amplitudes, integrals=integrals, couplings=couplings, virtual_energy=virtual_energy, sector_labels=sector_labels, sector_shift=sector_shift, occupied_energy=occupied_energy, pair_orbitals=pair_orbitals, third_orbitals=third_orbitals)


def virtual_levels(virtual_energy, sector_labels, sector_shift):
    match = sector_labels[:, None] == jnp.arange(NSECT, dtype=jnp.int32)[None, :]
    return virtual_energy + jnp.sum(jnp.where(match, sector_shift[None, :], jnp.zeros_like(sector_shift)[None, :]), axis=1)


def occupied_pick(occupied_energy, chosen):
    match = chosen[:, None] == jnp.arange(NOCC, dtype=jnp.int32)[None, :]
    return jnp.sum(jnp.where(match, occupied_energy[None, :], jnp.zeros_like(occupied_energy)[None, :]), axis=1)


def reference(amplitudes, integrals, couplings, virtual_energy, sector_labels, sector_shift, occupied_energy, pair_orbitals, third_orbitals):
    levels = virtual_levels(virtual_energy, sector_labels, sector_shift)
    pair_sum = jnp.sum(occupied_pick(occupied_energy, pair_orbitals))
    third = occupied_pick(occupied_energy, third_orbitals)
    block = min(A, 64)
    count = A // block
    amp_t = amplitudes.T
    level_blocks = levels.reshape(count, block)

    def one_k(total, kidx):
        slab = integrals[kidx].reshape(count, block, A, A)
        couple_slab = couplings[kidx].reshape(count, block, A, A)
        occ = pair_sum + third[kidx]

        def one_block(acc, pieces):
            vblock, ublock, level_b = pieces
            flat = vblock.reshape(block * A, A)
            product = jnp.dot(flat, amp_t, preferred_element_type=jnp.float32).astype(jnp.bfloat16).reshape(block, A, A)
            swapped = jnp.swapaxes(product, 1, 2)
            denom = occ - (level_b[:, None, None] + levels[None, :, None] + levels[None, None, :])
            triples = ((product.astype(jnp.float32) - swapped.astype(jnp.float32)) / denom).astype(jnp.bfloat16)
            return acc + jnp.dot(triples.reshape(block * A, A).T, ublock.reshape(block * A, A), preferred_element_type=jnp.float32), None

        total, _ = lax.scan(one_block, total, (slab, couple_slab, level_blocks))
        return total, None

    total, _ = lax.scan(one_k, jnp.zeros((A, A), jnp.float32), jnp.arange(K, dtype=jnp.int32))
    return total
```

```python
import functools

import jax
import jax.numpy as jnp
from jax import lax
from jax.experimental import pallas as pl
from jax.experimental.pallas import tpu as pltpu
from jax.sharding import PartitionSpec as P

NOCC = 64
NSECT = 8
BF16, F32 = jnp.bfloat16, jnp.float32
BOTH = ("bgrp", "clane")
NT = (((1,), (1,)), ((), ()))
NN = (((1,), (0,)), ((), ()))


def device(y, l, core, z, x):
    return (y * 4 + l * 2 + core) * 16 + z * 4 + x


GROUPS_YX = [
    [device(y, l, core, z, x) for y in range(4) for x in range(4)]
    for z in range(4) for l in range(2) for core in range(2)
]
GROUPS_ZC = [
    [device(y, l, core, z, x) for z in range(4) for l in range(2) for core in range(2)]
    for y in range(4) for x in range(4)
]


def exchange(values, groups):
    return lax.all_to_all(values, BOTH, 0, 0, axis_index_groups=groups, tiled=True)


def virtual_levels(virtual_energy, sector_labels, sector_shift):
    match = sector_labels[:, None] == jnp.arange(NSECT, dtype=jnp.int32)[None, :]
    return virtual_energy + jnp.sum(
        jnp.where(match, sector_shift[None, :], jnp.zeros_like(sector_shift)[None, :]), axis=1
    )


def occupied_pick(occupied_energy, chosen):
    match = chosen[:, None] == jnp.arange(NOCC, dtype=jnp.int32)[None, :]
    return jnp.sum(
        jnp.where(match, occupied_energy[None, :], jnp.zeros_like(occupied_energy)[None, :]), axis=1
    )


def spread_kernel(z_ref, amp_ref, out_ref):
    amp = amp_ref[...].astype(F32)
    wide = jnp.concatenate([amp] * 4, axis=1)
    lane = lax.broadcasted_iota(jnp.int32, wide.shape, 1)
    mine = (lane // 32) == z_ref[0]
    wide = jnp.where(mine, wide, jnp.zeros_like(wide)).astype(BF16)
    for d in range(16):
        out_ref[d] = wide


def gather_kernel(in_ref, out_ref):
    for q in range(4):
        total = in_ref[q].astype(F32)
        for z in range(1, 4):
            total = total + in_ref[4 * z + q].astype(F32)
        total = total.astype(BF16)
        for d in range(16):
            out_ref[d, pl.ds(32 * q, 32), :] = total


def reorder_kernel(in_ref, out_ref, rows_ref, cols_ref):
    @pl.when(pl.program_id(0) == 0)
    def _():
        to = lax.broadcasted_iota(jnp.int32, (512, 512), 0)
        of = lax.broadcasted_iota(jnp.int32, (512, 512), 1)
        rows_ref[...] = jnp.where(of == (to & 15) * 32 + (to >> 4), 1.0, 0.0).astype(BF16)
        src = ((of >> 5) & 3) * 128 + (of >> 7) * 32 + (of & 31)
        cols_ref[...] = jnp.where(to == src, 1.0, 0.0).astype(BF16)

    moved = lax.dot_general(rows_ref[...], in_ref[...], NN, preferred_element_type=F32).astype(BF16)
    moved = lax.dot_general(moved, cols_ref[...], NN, preferred_element_type=F32).astype(BF16)
    out_ref[...] = moved.reshape(32, 16, 512)


def reorder(values):
    return pl.pallas_call(
        reorder_kernel,
        out_shape=jax.ShapeDtypeStruct((32, 128, 512), BF16),
        grid=(8,),
        in_specs=[pl.BlockSpec((512, 512), lambda g: (g, 0))],
        out_specs=pl.BlockSpec((32, 16, 512), lambda g: (0, g, 0)),
        scratch_shapes=[pltpu.VMEM((512, 512), BF16), pltpu.VMEM((512, 512), BF16)],
        cost_estimate=pl.CostEstimate(flops=2**33, bytes_accessed=2**23, transcendentals=0),
    )(values)


SPLIT = 2


def send_kernel(amp_ref, ints_ref, out_ref, amp_full, wide):
    step = pl.program_id(0)
    rows = 512 // SPLIT

    @pl.when(step == 0)
    def _():
        for y in range(4):
            for x in range(4):
                amp_full[pl.ds(128 * y, 128), pl.ds(128 * x, 128)] = amp_ref[4 * y + x]

    mine = amp_full[pl.ds(pl.multiple_of(step * rows, rows), rows), :]
    for c in range(0, 32, 2):
        pair = ints_ref[pl.ds(c, 2)].reshape(256, 512)
        prod = lax.dot_general(mine, pair, NT, preferred_element_type=F32)
        wide[pl.ds(c, rows, stride=32), :] = prod[:, :128]
        wide[pl.ds(c + 1, rows, stride=32), :] = prod[:, 128:]

    def narrow(i, carry):
        at = pl.ds(pl.multiple_of(i * 512, 512), 512)
        out_ref[at, :] = wide[at, :].astype(BF16)
        return carry

    lax.fori_loop(0, rows * 32 // 512, narrow, 0)


def send_blocks(amp, ints):
    rows = 512 // SPLIT
    return pl.pallas_call(
        send_kernel,
        out_shape=jax.ShapeDtypeStruct((512 * 32, 128), BF16),
        grid=(SPLIT,),
        in_specs=[
            pl.BlockSpec((16, 128, 128), lambda g: (0, 0, 0)),
            pl.BlockSpec((32, 128, 512), lambda g: (0, 0, 0)),
        ],
        out_specs=pl.BlockSpec((rows * 32, 128), lambda g: (g, 0)),
        scratch_shapes=[pltpu.VMEM((512, 512), BF16), pltpu.VMEM((rows * 32, 128), F32)],
        cost_estimate=pl.CostEstimate(flops=2**31, bytes_accessed=2**23, transcendentals=0),
    )(amp, ints)


def own_kernel(amp_ref, ints_ref, out_ref, amp_full):
    @pl.when(pl.program_id(0) == 0)
    def _():
        for y in range(4):
            for x in range(4):
                amp_full[pl.ds(128 * y, 128), pl.ds(128 * x, 128)] = amp_ref[4 * y + x]

    for c in range(0, 4, 2):
        pair = ints_ref[pl.ds(c, 2)].reshape(256, 512)
        prod = lax.dot_general(amp_full[...], pair, NT, preferred_element_type=F32).astype(BF16)
        out_ref[c] = prod[:, :128]
        out_ref[c + 1] = prod[:, 128:]


def own_products(amp, ints):
    return pl.pallas_call(
        own_kernel,
        out_shape=jax.ShapeDtypeStruct((32, 512, 128), BF16),
        grid=(8,),
        in_specs=[
            pl.BlockSpec((16, 128, 128), lambda g: (0, 0, 0)),
            pl.BlockSpec((4, 128, 512), lambda g: (g, 0, 0)),
        ],
        out_specs=pl.BlockSpec((4, 512, 128), lambda g: (g, 0, 0)),
        scratch_shapes=[pltpu.VMEM((512, 512), BF16)],
        cost_estimate=pl.CostEstimate(flops=2**31, bytes_accessed=2**23, transcendentals=0),
    )(amp, ints)


CSTEP = 4


def fold_kernel(own_ref, came_ref, coup_ref, level_ref, shift_ref, out_ref, acc, trip):
    step = pl.program_id(0)
    for c in range(CSTEP):
        shift = shift_ref[pl.ds(step * CSTEP + c, 1), :]
        for i in range(16):
            at = pl.ds(32 * i, 32)
            gap = own_ref[c, at, :].astype(F32) - came_ref[i, c].astype(F32)
            denom = shift - level_ref[at, :]
            trip[at, pl.ds(128 * c, 128)] = (gap / denom).astype(BF16)
    part = lax.dot_general(
        trip[...], coup_ref[...].reshape(CSTEP * 128, 512), NN, preferred_element_type=F32
    )

    @pl.when(step == 0)
    def _():
        acc[...] = part

    @pl.when(step > 0)
    def _():
        acc[...] += part

    @pl.when(step == pl.num_programs(0) - 1)
    def _():
        for y in range(4):
            for x in range(4):
                out_ref[4 * y + x] = acc[pl.ds(128 * y, 128), pl.ds(128 * x, 128)].astype(BF16)


def fold(own, came, coup, level, shift):
    return pl.pallas_call(
        fold_kernel,
        out_shape=jax.ShapeDtypeStruct((16, 128, 128), BF16),
        grid=(32 // CSTEP,),
        in_specs=[
            pl.BlockSpec((CSTEP, 512, 128), lambda g: (g, 0, 0)),
            pl.BlockSpec((16, CSTEP, 32, 128), lambda g: (0, g, 0, 0)),
            pl.BlockSpec((CSTEP, 128, 512), lambda g: (g, 0, 0)),
            pl.BlockSpec((512, 128), lambda g: (0, 0)),
            pl.BlockSpec((32, 128), lambda g: (0, 0)),
        ],
        out_specs=pl.BlockSpec((16, 128, 128), lambda g: (0, 0, 0)),
        scratch_shapes=[pltpu.VMEM((512, 512), F32), pltpu.VMEM((512, CSTEP * 128), BF16)],
        cost_estimate=pl.CostEstimate(flops=2**31, bytes_accessed=12 * 2**20, transcendentals=0),
    )(own, came, coup, level, shift)


def first_sum_kernel(in_ref, out_ref):
    total = in_ref[0].astype(F32)
    for d in range(1, 16):
        total = total + in_ref[d].astype(F32)
    total = total.astype(BF16)
    for z in range(4):
        for q in range(4):
            out_ref[4 * z + q] = total[32 * q : 32 * q + 32]


def last_sum_kernel(z_ref, in_ref, out_ref):
    total = in_ref[0].astype(F32)
    for d in range(1, 16):
        total = total + in_ref[d].astype(F32)
    mine = jnp.zeros((32, 32), F32)
    for z in range(4):
        mine = jnp.where(z_ref[0] == z, total[:, 32 * z : 32 * z + 32], mine)
    out_ref[...] = mine


def small(kernel, shape, dtype, *args):
    specs = [
        pl.BlockSpec(memory_space=pltpu.SMEM if a.ndim == 1 else pltpu.VMEM) for a in args
    ]
    return pl.pallas_call(
        kernel,
        out_shape=jax.ShapeDtypeStruct(shape, dtype),
        in_specs=specs,
        out_specs=pl.BlockSpec(memory_space=pltpu.VMEM),
    )(*args)


def on_device(
    amplitudes,
    integrals,
    couplings,
    virtual_energy,
    sector_labels,
    sector_shift,
    occupied_energy,
    pair_orbitals,
    third_orbitals,
):
    z = (lax.axis_index("clane") // 4).astype(jnp.int32).reshape(1)

    amp = exchange(small(spread_kernel, (16, 32, 128), BF16, z, amplitudes), GROUPS_ZC)
    ints = reorder(integrals.reshape(4096, 512))
    amp = exchange(small(gather_kernel, (16, 128, 128), BF16, amp), GROUPS_YX)

    sent = send_blocks(amp, ints)
    came = lax.all_to_all(sent.reshape(16, 1024, 128), "clane", 0, 0, tiled=True)

    _, couplings, amp2, small_in = lax.optimization_barrier(
        (sent, couplings, amp,
         (virtual_energy, sector_labels, sector_shift, occupied_energy, pair_orbitals, third_orbitals))
    )
    virtual_energy, sector_labels, sector_shift, occupied_energy, pair_orbitals, third_orbitals = small_in
    own = own_products(amp2, ints)
    coup = reorder(couplings.reshape(4096, 512))
    levels = virtual_levels(virtual_energy, sector_labels, sector_shift)
    level_b = lax.dynamic_slice_in_dim(levels, lax.axis_index("bgrp") * 32, 32)
    level_c = lax.dynamic_slice_in_dim(levels, lax.axis_index("clane") * 32, 32)
    occ = jnp.sum(occupied_pick(occupied_energy, pair_orbitals)) + occupied_pick(
        occupied_energy, third_orbitals
    )
    lanes = (occ[:, None] - level_b[None, :]).reshape(1, 128)
    shift = lanes - level_c[:, None]
    level = jnp.broadcast_to(levels[:, None], (512, 128))

    parts = fold(own, came.reshape(16, 32, 32, 128), coup, level, shift)
    parts = exchange(parts, GROUPS_YX)
    parts = exchange(small(first_sum_kernel, (16, 32, 128), BF16, parts), GROUPS_ZC)
    return small(last_sum_kernel, (32, 32), F32, z, parts)


def solution(mesh):
    in_specs = (
        P("bgrp", "clane"),
        P(None, "bgrp", "clane", None),
        P(None, "bgrp", "clane", None),
        P(),
        P(),
        P(),
        P(),
        P(),
        P(),
    )
    out_specs = P("bgrp", "clane")
    return jax.shard_map(
        on_device, mesh=mesh, in_specs=in_specs, out_specs=out_specs, check_vma=False
    )
```

```python
import functools

import jax
import jax.numpy as jnp
from jax import lax
from jax.experimental import pallas as pl
from jax.experimental.pallas import tpu as pltpu
from jax.sharding import PartitionSpec as P

NOCC = 64
NSECT = 8
BF16, F32 = jnp.bfloat16, jnp.float32
BOTH = ("bgrp", "clane")
NT = (((1,), (1,)), ((), ()))
NN = (((1,), (0,)), ((), ()))


def device(y, l, core, z, x):
    return (y * 4 + l * 2 + core) * 16 + z * 4 + x


GROUPS_YX = [
    [device(y, l, core, z, x) for y in range(4) for x in range(4)]
    for z in range(4) for l in range(2) for core in range(2)
]
GROUPS_ZC = [
    [device(y, l, core, z, x) for z in range(4) for l in range(2) for core in range(2)]
    for y in range(4) for x in range(4)
]


def exchange(values, groups):
    return lax.all_to_all(values, BOTH, 0, 0, axis_index_groups=groups, tiled=True)


def virtual_levels(virtual_energy, sector_labels, sector_shift):
    match = sector_labels[:, None] == jnp.arange(NSECT, dtype=jnp.int32)[None, :]
    return virtual_energy + jnp.sum(
        jnp.where(match, sector_shift[None, :], jnp.zeros_like(sector_shift)[None, :]), axis=1
    )


def occupied_pick(occupied_energy, chosen):
    match = chosen[:, None] == jnp.arange(NOCC, dtype=jnp.int32)[None, :]
    return jnp.sum(
        jnp.where(match, occupied_energy[None, :], jnp.zeros_like(occupied_energy)[None, :]), axis=1
    )


def spread_kernel(z_ref, amp_ref, out_ref):
    amp = amp_ref[...].astype(F32)
    wide = jnp.concatenate([amp] * 4, axis=1)
    lane = lax.broadcasted_iota(jnp.int32, wide.shape, 1)
    mine = (lane // 32) == z_ref[0]
    wide = jnp.where(mine, wide, jnp.zeros_like(wide)).astype(BF16)
    for d in range(16):
        out_ref[d] = wide


def gather_kernel(in_ref, out_ref):
    for q in range(4):
        total = in_ref[q].astype(F32)
        for z in range(1, 4):
            total = total + in_ref[4 * z + q].astype(F32)
        total = total.astype(BF16)
        for d in range(16):
            out_ref[d, pl.ds(32 * q, 32), :] = total


def reorder_kernel(in_ref, out_ref, rows_ref, cols_ref):
    @pl.when(pl.program_id(0) == 0)
    def _():
        to = lax.broadcasted_iota(jnp.int32, (512, 512), 0)
        of = lax.broadcasted_iota(jnp.int32, (512, 512), 1)
        rows_ref[...] = jnp.where(of == (to & 15) * 32 + (to >> 4), 1.0, 0.0).astype(BF16)
        src = ((of >> 5) & 3) * 128 + (of >> 7) * 32 + (of & 31)
        cols_ref[...] = jnp.where(to == src, 1.0, 0.0).astype(BF16)

    moved = lax.dot_general(rows_ref[...], in_ref[...], NN, preferred_element_type=F32).astype(BF16)
    moved = lax.dot_general(moved, cols_ref[...], NN, preferred_element_type=F32).astype(BF16)
    out_ref[...] = moved.reshape(32, 16, 512)


def reorder(values):
    return pl.pallas_call(
        reorder_kernel,
        out_shape=jax.ShapeDtypeStruct((32, 128, 512), BF16),
        grid=(8,),
        in_specs=[pl.BlockSpec((512, 512), lambda g: (g, 0))],
        out_specs=pl.BlockSpec((32, 16, 512), lambda g: (0, g, 0)),
        scratch_shapes=[pltpu.VMEM((512, 512), BF16), pltpu.VMEM((512, 512), BF16)],
        compiler_params=pltpu.CompilerParams(vmem_limit_bytes=16 * 2**20),
        cost_estimate=pl.CostEstimate(flops=2**33, bytes_accessed=2**23, transcendentals=0),
    )(values)


WAVES = (
    ((2, 0), (2, 1), (2, 2), (2, 3)),
    ((1, 0), (3, 0), (1, 2), (3, 2)),
    ((1, 1), (3, 1), (1, 3), (3, 3)),
    ((0, 0), (0, 1), (0, 2), (0, 3)),
)
FOLDS = (0, 3, 1, 2)


def hop(dz, dx):
    return [
        (4 * z + x, 4 * ((z + dz) % 4) + (x + dx) % 4) for z in range(4) for x in range(4)
    ]


def send_kernel(group, at_ref, amp_ref, ints_ref, *refs, CS):
    outs, own_ref, lhs, wide = refs[:4], refs[4], refs[5], refs[6]
    step = pl.program_id(0)

    @pl.when(step == 0)
    def _():
        for m, (dz, dx) in enumerate(group):
            z, x = (at_ref[0] + dz) & 3, (at_ref[1] + dx) & 3
            for col in range(4):
                lhs[pl.ds(32 * m, 32), pl.ds(128 * col, 128)] = amp_ref[
                    4 * z + col, pl.ds(pl.multiple_of(32 * x, 32), 32), :]

    for c in range(0, CS, 2):
        pair = ints_ref[pl.ds(c, 2)].reshape(256, 512)
        prod = lax.dot_general(lhs[...], pair, NT, preferred_element_type=F32)
        base = step * CS + c
        wide[pl.ds(base, 128, stride=32), :] = prod[:, :128]
        wide[pl.ds(base + 1, 128, stride=32), :] = prod[:, 128:]
        own_ref[c] = prod[:, :128].astype(BF16)
        own_ref[c + 1] = prod[:, 128:].astype(BF16)

    @pl.when(step == pl.num_programs(0) - 1)
    def _():
        for m in range(4):
            def narrow(i, carry, m=m):
                n = 256
                outs[m][pl.ds(pl.multiple_of(i * n, n), n), :] = wide[
                    pl.ds(pl.multiple_of(m * 1024 + i * n, n), n), :].astype(BF16)
                return carry
            lax.fori_loop(0, 4, narrow, 0)

def send(group, at, amp, ints, CS=8):
    return pl.pallas_call(
        functools.partial(send_kernel, group, CS=CS),
        out_shape=[jax.ShapeDtypeStruct((1024, 128), BF16)] * 4
        + [jax.ShapeDtypeStruct((32, 128, 128), BF16)],
        grid=(32 // CS,),
        in_specs=[
            pl.BlockSpec(memory_space=pltpu.SMEM),
            pl.BlockSpec((16, 128, 128), lambda g: (0, 0, 0)),
            pl.BlockSpec((CS, 128, 512), lambda g: (g, 0, 0)),
        ],
        out_specs=[pl.BlockSpec((1024, 128), lambda g: (0, 0))] * 4
        + [pl.BlockSpec((CS, 128, 128), lambda g: (g, 0, 0))],
        scratch_shapes=[pltpu.VMEM((128, 512), BF16), pltpu.VMEM((4096, 128), F32)],
        compiler_params=pltpu.CompilerParams(vmem_limit_bytes=20 * 2**20),
        cost_estimate=pl.CostEstimate(flops=2**29, bytes_accessed=6 * 2**20, transcendentals=0),
    )(at, amp, ints)

def fold_kernel(group, last, at_ref, own_ref, c0, c1, c2, c3, coup_ref, level_ref, shift_ref, *refs, FS):
    if last:
        pieces, (out_ref, acc, trip) = refs[:3], refs[3:]
    else:
        out_ref, acc, trip = refs
    came = (c0, c1, c2, c3)
    step = pl.program_id(0)
    place = []
    for m, (dz, dx) in enumerate(group):
        place.append(((at_ref[0] - dz) & 3, (at_ref[1] - dx) & 3))
    for c in range(FS):
        shift = shift_ref[pl.ds(step * FS + c, 1), :]
        for m in range(4):
            z, x = place[m]
            neg = group.index(((-group[m][0]) % 4, (-group[m][1]) % 4))
            gap = own_ref[c, pl.ds(32 * neg, 32), :].astype(F32) - came[m][c].astype(F32)
            denom = shift - level_ref[pl.ds(pl.multiple_of(128 * z + 32 * x, 32), 32), :]
            trip[pl.ds(32 * m, 32), pl.ds(128 * c, 128)] = (gap / denom).astype(BF16)
    part = lax.dot_general(
        trip[...], coup_ref[...].reshape(FS * 128, 512), NN, preferred_element_type=F32)

    @pl.when(step == 0)
    def _():
        acc[...] = part

    @pl.when(step > 0)
    def _():
        acc[...] += part

    @pl.when(step == pl.num_programs(0) - 1)
    def _():
        if not last:
            for m in range(4):
                for x in range(4):
                    out_ref[m, x] = acc[pl.ds(32 * m, 32), pl.ds(128 * x, 128)].astype(BF16)
        else:
            for g, piece in last:
                for m, (dz, dx) in enumerate(g):
                    z, x = (at_ref[0] - dz) & 3, (at_ref[1] - dx) & 3
                    for col in range(4):
                        out_ref[4 * z + col, pl.ds(pl.multiple_of(32 * x, 32), 32), :] = pieces[piece][m, col]
            for m in range(4):
                z, x = place[m]
                for col in range(4):
                    out_ref[4 * z + col, pl.ds(pl.multiple_of(32 * x, 32), 32), :] = acc[
                        pl.ds(32 * m, 32), pl.ds(128 * col, 128)].astype(BF16)

def fold(group, at, own, came, coup, level, shift, last=(), FS=4):
    pieces = [p for _, p in last]
    lastspec = tuple((g, i) for i, (g, _) in enumerate(last))
    full = lambda *s: pl.BlockSpec(s, lambda g: (0,) * len(s))
    return pl.pallas_call(
        functools.partial(fold_kernel, group, lastspec, FS=FS),
        out_shape=jax.ShapeDtypeStruct((16, 128, 128) if last else (4, 4, 32, 128), BF16),
        grid=(32 // FS,),
        in_specs=[pl.BlockSpec(memory_space=pltpu.SMEM),
            pl.BlockSpec((FS, 128, 128), lambda g: (g, 0, 0))]
        + [pl.BlockSpec((FS, 32, 128), lambda g: (g, 0, 0))] * 4
        + [pl.BlockSpec((FS, 128, 512), lambda g: (g, 0, 0)), full(512, 128), full(32, 128)]
        + [full(4, 4, 32, 128)] * len(pieces),
        out_specs=full(16, 128, 128) if last else full(4, 4, 32, 128),
        scratch_shapes=[pltpu.VMEM((128, 512), F32), pltpu.VMEM((128, FS * 128), BF16)],
        compiler_params=pltpu.CompilerParams(vmem_limit_bytes=20 * 2**20),
        cost_estimate=pl.CostEstimate(flops=2**29, bytes_accessed=6 * 2**20, transcendentals=0),
    )(at, own, *[v.reshape(32, 32, 128) for v in came], coup, level, shift, *pieces)


def first_sum_kernel(in_ref, out_ref):
    total = in_ref[0].astype(F32)
    for d in range(1, 16):
        total = total + in_ref[d].astype(F32)
    total = total.astype(BF16)
    for z in range(4):
        for q in range(4):
            out_ref[4 * z + q] = total[32 * q : 32 * q + 32]


def last_sum_kernel(z_ref, in_ref, out_ref):
    total = in_ref[0].astype(F32)
    for d in range(1, 16):
        total = total + in_ref[d].astype(F32)
    mine = jnp.zeros((32, 32), F32)
    for z in range(4):
        mine = jnp.where(z_ref[0] == z, total[:, 32 * z : 32 * z + 32], mine)
    out_ref[...] = mine


def small(kernel, shape, dtype, *args):
    specs = [
        pl.BlockSpec(memory_space=pltpu.SMEM if a.ndim == 1 else pltpu.VMEM) for a in args
    ]
    return pl.pallas_call(
        kernel,
        out_shape=jax.ShapeDtypeStruct(shape, dtype),
        in_specs=specs,
        out_specs=pl.BlockSpec(memory_space=pltpu.VMEM),
        compiler_params=pltpu.CompilerParams(vmem_limit_bytes=4 * 2**20),
    )(*args)


def on_device(
    amplitudes,
    integrals,
    couplings,
    virtual_energy,
    sector_labels,
    sector_shift,
    occupied_energy,
    pair_orbitals,
    third_orbitals,
):
    lane = lax.axis_index("clane").astype(jnp.int32)
    z = (lane // 4).reshape(1)
    at = jnp.stack([lane // 4, lane % 4])

    amp = exchange(small(spread_kernel, (16, 32, 128), BF16, z, amplitudes), GROUPS_ZC)
    ints = reorder(integrals.reshape(4096, 512))
    amp = exchange(small(gather_kernel, (16, 128, 128), BF16, amp), GROUPS_YX)

    coup = reorder(couplings.reshape(4096, 512))
    own, came = [], []
    for wave in WAVES:
        *sent, mine = send(wave, at, amp, ints, CS=16)
        amp, _ = lax.optimization_barrier((amp, mine))
        own.append(mine)
        came.append(
            [
                lax.ppermute(s, "clane", hop(*move)) if move != (0, 0) else s
                for s, move in zip(sent, wave)
            ]
        )

    levels = virtual_levels(virtual_energy, sector_labels, sector_shift)
    level_b = lax.dynamic_slice_in_dim(levels, lax.axis_index("bgrp") * 32, 32)
    level_c = lax.dynamic_slice_in_dim(levels, lax.axis_index("clane") * 32, 32)
    occ = jnp.sum(occupied_pick(occupied_energy, pair_orbitals)) + occupied_pick(
        occupied_energy, third_orbitals
    )
    lanes = (occ[:, None] - level_b[None, :]).reshape(1, 128)
    shift = lanes - level_c[:, None]
    level = jnp.broadcast_to(levels[:, None], (512, 128))

    pieces = []
    for w in FOLDS:
        last = pieces if w == FOLDS[-1] else ()
        parts = fold(WAVES[w], at, own[w], came[w], coup, level, shift, last=last, FS=16)
        pieces.append((WAVES[w], parts))
    parts = exchange(parts, GROUPS_YX)
    parts = exchange(small(first_sum_kernel, (16, 32, 128), BF16, parts), GROUPS_ZC)
    return small(last_sum_kernel, (32, 32), F32, z, parts)


def solution(mesh):
    in_specs = (
        P("bgrp", "clane"),
        P(None, "bgrp", "clane", None),
        P(None, "bgrp", "clane", None),
        P(),
        P(),
        P(),
        P(),
        P(),
        P(),
    )
    out_specs = P("bgrp", "clane")
    return jax.shard_map(
        on_device, mesh=mesh, in_specs=in_specs, out_specs=out_specs, check_vma=False
    )
```
